32 devices in a mesh: section: 2 (over core), seq: 16 (over z, y, x).
Axes of the slice: x: 2, y: 2, z: 4, core: 2. Of those that a mesh axis runs over, the one named last changes fastest.
Arguments:
- fields: bfloat16 [8, 2048, 2048], P(None, 'seq'), may hold values from -6 to 6
- cotangent: bfloat16 [2, 2048, 2048], P(None, 'seq'), may hold values from -0.08984375 to 0.08984375
- assignment: int32 [8], replicated, may hold values from 0 to 7, each once
- norm_gain: float32 [2, 2048], P('section'), may hold values from 0.1 to 1.9
- value_inner: bfloat16 [2, 16, 128, 128], P('section'), may hold values from -0.5 to 0.5
- value_outer: bfloat16 [2, 16, 16, 128], P('section'), may hold values from -1.5 to 1.5
- gate_inner: bfloat16 [2, 16, 128, 128], P('section'), may hold values from -0.5 to 0.5
- gate_outer: bfloat16 [2, 16, 16, 128], P('section'), may hold values from -1.5 to 1.5
- seq_inner: bfloat16 [2, 16, 128, 128], P('section', 'seq'), may hold values from -0.5 to 0.5
- seq_outer: bfloat16 [2, 128, 16, 16], P('section', 'seq'), may hold values from -1.5 to 1.5
Outputs:
- final_rows: bfloat16 [2, 2048, 2048], P(None, 'seq')
- grad_gain: float32 [2, 2048], P('section')
- grad_value_inner: float32 [2, 16, 128, 128], P('section')
- grad_value_outer: float32 [2, 16, 16, 128], P('section')
- grad_gate_inner: float32 [2, 16, 128, 128], P('section')
- grad_gate_outer: float32 [2, 16, 16, 128], P('section')
- grad_seq_inner: float32 [2, 16, 128, 128], P('section', 'seq')
- grad_seq_outer: float32 [2, 128, 16, 16], P('section', 'seq')
The draws below stay inside these ranges and needn't reach their ends.
Inputs may be any that keep to these rules, and one draw needn't show every extreme that they name: `assignment`: a permutation of 0 to 7.
All inputs are finite; a program needn't handle non-finite values.
Results may differ from the reference program's by a relative error of at most 0.029.
Values may be sent and summed in bfloat16 or wider, within the bound.
A program may use at most 128 MiB of HBM per device.

```python
import jax
import jax.numpy as jnp
from jax import lax

D = 2048
WB = 128
BS = 128
MB = 2
NF = 8
L = 2048
NB = 16
KB = 16
N_SECTION = 2


def steps_of(stream_key, extent, shards, low, largest):
    level = 1.0
    for dim, shards_of in shards:
        heights = jax.random.uniform(jax.random.fold_in(jax.random.fold_in(stream_key, 6), dim), (shards_of,), jnp.float32, low / len(shards), largest / len(shards))
        level = level * jnp.repeat(jnp.exp(heights), extent[dim] // shards_of).reshape((-1,) + (1,) * (len(extent) - 1 - dim))
    return level


def normal_values(key, shape, width, most, pieces=(), held_as=jnp.bfloat16):
    loudness = steps_of(key, shape, pieces, -0.22, 0.18) if pieces else 1.0
    entries = jax.random.normal(key, shape, jnp.float32) * width * loudness
    return jnp.minimum(jnp.maximum(entries, -most), most).astype(held_as)


def setup_inputs(seed: int = 0) -> dict:
    keys = jax.random.split(jax.random.key(seed), 11)
    fields = normal_values(keys[0], (NF, L, D), 1.0, 6.0, ((1, 16),))
    cotangent = normal_values(keys[1], (MB, L, D), 0.015, 0.08984375, ((1, 16),))
    assignment = jax.random.permutation(keys[2], NF).astype(jnp.int32)
    norm_gain = jnp.clip(1.0 + 0.18 * jax.random.normal(keys[3], (N_SECTION, D), jnp.float32), 0.1, 1.9)
    value_inner = normal_values(keys[4], (N_SECTION, KB, WB, WB), WB ** -0.5, 0.5, ((0, 2),))
    value_outer = normal_values(keys[5], (N_SECTION, KB, KB, WB), KB ** -0.5, 1.5, ((0, 2),))
    gate_inner = normal_values(keys[6], (N_SECTION, KB, WB, WB), WB ** -0.5, 0.5, ((0, 2),))
    gate_outer = normal_values(keys[7], (N_SECTION, KB, KB, WB), KB ** -0.5, 1.5, ((0, 2),))
    seq_inner = normal_values(keys[8], (N_SECTION, NB, BS, BS), BS ** -0.5, 0.5, ((0, 2), (1, 16)))
    seq_outer = normal_values(keys[9], (N_SECTION, BS, NB, NB), NB ** -0.5, 1.5, ((0, 2), (1, 16)))
    return dict(fields=fields, cotangent=cotangent, assignment=assignment, norm_gain=norm_gain, value_inner=value_inner, value_outer=value_outer, gate_inner=gate_inner, gate_outer=gate_outer, seq_inner=seq_inner, seq_outer=seq_outer)


EPSILON = 1e-06

def width_mix(hidden, inner, outer):
    count = hidden.shape[0]
    blocks = hidden.reshape(count, KB, WB).astype(jnp.float32)
    middle = jnp.einsum('nkj,kjq->nkq', blocks, inner.astype(jnp.float32)).astype(jnp.bfloat16)
    mixed = jnp.einsum('nkq,klq->nlq', middle.astype(jnp.float32), outer.astype(jnp.float32))
    return (mixed.reshape(count, D).astype(jnp.bfloat16), middle)

def width_back(hidden, middle, inner, outer, upstream):
    count = hidden.shape[0]
    blocks = hidden.reshape(count, KB, WB).astype(jnp.float32)
    up_blocks = upstream.reshape(count, KB, WB).astype(jnp.float32)
    grad_outer = jnp.einsum('nkq,nlq->klq', middle.astype(jnp.float32), up_blocks)
    grad_middle = jnp.einsum('nlq,klq->nkq', up_blocks, outer.astype(jnp.float32)).astype(jnp.bfloat16)
    grad_inner = jnp.einsum('nkj,nkq->kjq', blocks, grad_middle.astype(jnp.float32))
    grad_hidden = jnp.einsum('nkq,kjq->nkj', grad_middle.astype(jnp.float32), inner.astype(jnp.float32))
    return (grad_hidden.reshape(count, D), grad_inner, grad_outer)

def front(inputs, weights):
    wide = inputs.astype(jnp.float32)
    factor = lax.rsqrt(lax.optimization_barrier(jnp.mean(wide * wide, axis=-1, keepdims=True)) + EPSILON)
    hidden = (wide * factor * weights[0]).astype(jnp.bfloat16)
    values, value_mid = width_mix(hidden, weights[1], weights[2])
    gates, gate_mid = width_mix(hidden, weights[3], weights[4])
    return (wide, factor, hidden, values, value_mid, gates, gate_mid)

def seq_forward(values, weights):
    blocks = values.reshape(-1, BS, D).astype(jnp.float32)
    first_mix = jnp.einsum('bpi,bic->bpc', weights[5].astype(jnp.float32), blocks).astype(jnp.bfloat16)
    second = jnp.einsum('ipb,bic->pic', weights[6].astype(jnp.float32), first_mix.astype(jnp.float32))
    return (first_mix, second.astype(jnp.bfloat16).reshape(-1, D))

def layer(inputs, weights):
    wide, factor, hidden, values, value_mid, gates, gate_mid = front(inputs, weights)
    first_mix, mixed = seq_forward(values, weights)
    return (wide + mixed.astype(jnp.float32) * gates.astype(jnp.float32)).astype(jnp.bfloat16)

def layer_back(inputs, upstream, weights):
    wide, factor, hidden, values, value_mid, gates, gate_mid = front(inputs, weights)
    first_mix, mixed = seq_forward(values, weights)
    up_wide = upstream.astype(jnp.float32)
    grad_mixed = (up_wide * gates.astype(jnp.float32)).astype(jnp.bfloat16)
    grad_gates = (up_wide * mixed.astype(jnp.float32)).astype(jnp.bfloat16)
    grad_blocks = grad_mixed.reshape(-1, BS, D).astype(jnp.float32)
    grad_first = jnp.einsum('ipb,pic->bic', weights[6].astype(jnp.float32), grad_blocks).astype(jnp.bfloat16)
    grad_sout = jnp.einsum('pic,bic->ipb', grad_blocks, first_mix.astype(jnp.float32))
    grad_values = jnp.einsum('bpi,bpc->bic', weights[5].astype(jnp.float32), grad_first.astype(jnp.float32))
    grad_values = grad_values.astype(jnp.bfloat16).reshape(-1, D)
    grad_sin = jnp.einsum('bpc,bic->bpi', grad_first.astype(jnp.float32), values.reshape(-1, BS, D).astype(jnp.float32))
    hidden_v, grad_vin, grad_vout = width_back(hidden, value_mid, weights[1], weights[2], grad_values)
    hidden_g, grad_gin, grad_gout = width_back(hidden, gate_mid, weights[3], weights[4], grad_gates)
    grad_hidden = hidden_v + hidden_g
    grad_norm = lax.optimization_barrier(jnp.sum(grad_hidden * wide * factor, axis=0))
    scaled = weights[0] * grad_hidden
    grad_input = up_wide + factor * scaled - wide * factor ** 3 * lax.optimization_barrier(jnp.mean(scaled * wide, axis=-1, keepdims=True))
    return (grad_input.astype(jnp.bfloat16), (grad_norm, grad_vin, grad_vout, grad_gin, grad_gout, grad_sin, grad_sout))

def reference(fields, cotangent, assignment, norm_gain, value_inner, value_outer, gate_inner, gate_outer, seq_inner, seq_outer):
    arrays = (norm_gain, value_inner, value_outer, gate_inner, gate_outer, seq_inner, seq_outer)
    weights_zero = tuple((item[0] for item in arrays))
    weights_one = tuple((item[1] for item in arrays))
    sums_zero = tuple((jnp.zeros(item.shape[1:], jnp.float32) for item in arrays))
    sums_one = tuple((jnp.zeros(item.shape[1:], jnp.float32) for item in arrays))
    finals = []
    for micro in range(MB):
        start = fields[assignment[micro]]
        middle = layer(start, weights_zero)
        finals.append(layer(middle, weights_one))
        back_one, grads_one = layer_back(middle, cotangent[micro], weights_one)
        back_zero, grads_zero = layer_back(start, back_one, weights_zero)
        sums_one = tuple((total + part for total, part in zip(sums_one, grads_one)))
        sums_zero = tuple((total + part for total, part in zip(sums_zero, grads_zero)))
    stacked = tuple((jnp.stack([first, second]) for first, second in zip(sums_zero, sums_one)))
    return (jnp.stack(finals), stacked[0], stacked[1], stacked[2], stacked[3], stacked[4], stacked[5], stacked[6])
```

```python
import functools

import jax
import jax.numpy as jnp
from jax import lax
from jax.experimental import pallas as pl
from jax.experimental.pallas import tpu as pltpu
from jax.sharding import PartitionSpec as P

D = 2048
WB = 128
BS = 128
KB = 16
EPSILON = 1e-06
F32 = jnp.float32
BF16 = jnp.bfloat16
MESH = pl.DeviceIdType.MESH
VMEM = pl.BlockSpec(memory_space=pltpu.VMEM)
WIDE = 512


def dot(a, b, ca, cb):
    return lax.dot_general(a, b, (((ca,), (cb,)), ((), ())), preferred_element_type=F32)


def lane(k):
    return pl.ds(pl.multiple_of(k * WB, WB), WB)


def greet(n, me):
    barrier = pltpu.get_barrier_semaphore()

    def one(d, c):
        pl.semaphore_signal(
            barrier, inc=1, device_id={"seq": lax.rem(me + d, n)}, device_id_type=MESH
        )
        return c

    lax.fori_loop(1, n, one, 0)


def greeted(n):
    pl.semaphore_wait(pltpu.get_barrier_semaphore(), n - 1)


def piece(src, dst, sems, row, to, at, d):
    return pltpu.make_async_remote_copy(
        src_ref=src.at[row],
        dst_ref=dst.at[at],
        send_sem=sems[0].at[d],
        recv_sem=sems[1].at[d],
        device_id={"seq": to},
        device_id_type=MESH,
    )


def send_all(n, me, src, dst, sems):
    def one(d, c):
        peer = lax.rem(me + d, n)
        piece(src, dst, sems, peer, peer, me, d).start()
        return c

    lax.fori_loop(1, n, one, 0)
    dst[me] = src[me]


def wait_all(n, me, src, dst, sems):
    def one(d, c):
        peer = lax.rem(me + d, n)
        origin = lax.rem(me + n - d, n)
        copy = piece(src, dst, sems, peer, peer, origin, d)
        copy.wait_send()
        copy.wait_recv()
        return c

    lax.fori_loop(1, n, one, 0)


def cross(read, write, b_ref, back):
    def rows(i, c):
        at = pl.ds(pl.multiple_of(i * 16, 16), 16)
        parts = [read(k, at).astype(F32) for k in range(KB)]
        for l in range(KB):
            total = None
            for k in range(KB):
                row = b_ref[l, k : k + 1, :] if back else b_ref[k, l : l + 1, :]
                term = parts[k] * row
                total = term if total is None else total + term
            write(l, at, total.astype(BF16))
        return c

    lax.fori_loop(0, BS // 16, rows, 0)


def row_factor(x_ref):
    wide = x_ref[...].astype(F32)
    return lax.rsqrt(jnp.mean(wide * wide, axis=-1, keepdims=True) + EPSILON)


def spread_rows(n, rows, dtype=BF16):
    pad = rows // n
    each = BS // n
    at = lax.broadcasted_iota(jnp.int32, (rows, BS), 0)
    to = lax.broadcasted_iota(jnp.int32, (rows, BS), 1)
    hit = (at // pad * each + at % pad == to) & (at % pad < each)
    return jnp.where(hit, 1.0, 0.0).astype(dtype)


def fwd_kernel(
    n, x_ref, gain_ref, w_ref, vo_ref, go_ref, sin_ref, sx_ref,
    out_ref, h_ref, t_ref, v_ref, g_ref, sp_ref, s_ref,
    a1, b1, a2, b2, ss1, rs1, ss2, rs2,
):
    me = lax.axis_index("seq")
    rows = sin_ref.shape[0]
    pad = rows // n
    greet(n, me)
    factor = row_factor(x_ref)
    for k in range(KB):
        cols = slice(k * WB, (k + 1) * WB)
        gain = gain_ref[k : k + 1, :]
        hidden = (x_ref[:, cols].astype(F32) * factor * gain).astype(BF16)
        h_ref[:, cols] = hidden
        t_ref[k] = dot(hidden, w_ref[k], 1, 0).astype(BF16)

    def put(ref):
        def write(l, at, value):
            ref[at, l * WB : (l + 1) * WB] = value

        return write

    cross(lambda k, at: t_ref[k, at, :WB], put(v_ref), vo_ref, False)
    for c in range(0, D, WIDE):
        y = dot(sin_ref[...], v_ref[:, c : c + WIDE], 1, 0)
        a1[:, :, c : c + WIDE] = y.reshape(n, pad, WIDE).astype(BF16)
    greeted(n)
    send_all(n, me, a1, b1, (ss1, rs1))
    cross(lambda k, at: t_ref[k, at, WB:], put(g_ref), go_ref, False)
    wait_all(n, me, a1, b1, (ss1, rs1))
    for c in range(0, D, WIDE):
        got = b1[:, :, c : c + WIDE].astype(F32).reshape(rows, WIDE).astype(BF16)
        sp_ref[:, c : c + WIDE] = got
        y = dot(sx_ref[...], got, 1, 0)
        a2[:, :, c : c + WIDE] = y.reshape(n, pad, WIDE).astype(BF16)
    send_all(n, me, a2, b2, (ss2, rs2))
    wait_all(n, me, a2, b2, (ss2, rs2))
    for c in range(0, D, WIDE):
        cols = slice(c, c + WIDE)
        mixed = b2[:, :, cols].astype(F32).reshape(rows, WIDE)
        if rows != BS:
            mixed = dot(spread_rows(n, rows), mixed.astype(BF16), 0, 0)
        s_ref[:, cols] = mixed.astype(BF16)
        out_ref[:, cols] = (
            x_ref[:, cols].astype(F32) + mixed * g_ref[:, cols].astype(F32)
        ).astype(BF16)


def bwd_kernel(
    n, e_ref, x_ref, h_ref, t_ref, v_ref, g_ref, sp_ref, s_ref,
    gain_ref, w_ref, vo_ref, go_ref, sin_ref, sx_ref,
    dx_ref, egain_ref, ew_ref, evo_ref, ego_ref, esin_ref, esx_ref,
    a1, b1, a2, b2, dt, up, dh, ss1, rs1, ss2, rs2,
):
    me = lax.axis_index("seq")
    rows = sin_ref.shape[0]
    pad = rows // n
    greet(n, me)
    for c in range(0, D, WIDE):
        cols = slice(c, c + WIDE)
        ds = e_ref[:, cols].astype(F32) * g_ref[:, cols].astype(F32)
        if rows != BS:
            ds = dot(spread_rows(n, rows), ds.astype(BF16), 1, 0)
        a1[:, :, cols] = ds.reshape(n, pad, WIDE).astype(BF16)
    greeted(n)
    send_all(n, me, a1, b1, (ss1, rs1))

    def outer_back(first, b_ref, eb_ref):
        def write(k, at, value):
            dt[k, at, first : first + WB] = value

        cross(lambda l, at: up[at, l * WB : (l + 1) * WB], write, b_ref, True)

        def block(k, c):
            middle = t_ref[k, :, first : first + WB].astype(F32)
            for l in range(KB):
                both = middle * up[:, l * WB : (l + 1) * WB]
                eb_ref[k, l : l + 1, :] = jnp.sum(both, axis=0, keepdims=True)
            return c

        lax.fori_loop(0, KB, block, 0)

    for c in range(0, D, WIDE):
        cols = slice(c, c + WIDE)
        dg = e_ref[:, cols].astype(F32) * s_ref[:, cols].astype(F32)
        up[:, cols] = dg.astype(BF16).astype(F32)
    wait_all(n, me, a1, b1, (ss1, rs1))
    pairs = jnp.zeros((rows, rows), F32)
    for c in range(0, D, WIDE):
        cols = slice(c, c + WIDE)
        got = b1[:, :, cols].astype(F32).reshape(rows, WIDE).astype(BF16)
        y = dot(sx_ref[...], got, 0, 0)
        a2[:, :, cols] = y.reshape(n, pad, WIDE).astype(BF16)
    send_all(n, me, a2, b2, (ss2, rs2))
    for c in range(0, D, WIDE):
        cols = slice(c, c + WIDE)
        got = b1[:, :, cols].astype(F32).reshape(rows, WIDE).astype(BF16)
        pairs += dot(got, sp_ref[:, cols], 1, 1)
    esx_ref[...] = pairs
    outer_back(WB, go_ref, ego_ref)
    wait_all(n, me, a2, b2, (ss2, rs2))
    inner = jnp.zeros((rows, BS), F32)
    for c in range(0, D, WIDE):
        cols = slice(c, c + WIDE)
        dy = b2[:, :, cols].astype(F32).reshape(rows, WIDE).astype(BF16)
        inner += dot(dy, v_ref[:, cols], 1, 1)
        up[:, cols] = dot(sin_ref[...], dy, 0, 0).astype(BF16).astype(F32)
    esin_ref[...] = inner
    outer_back(0, vo_ref, evo_ref)
    factor = row_factor(x_ref)
    lean = jnp.zeros((BS, WB), F32)
    for k in range(KB):
        cols = slice(k * WB, (k + 1) * WB)
        both = dt[k]
        ew_ref[k] = dot(h_ref[:, cols], both, 0, 0)
        part = dot(both, w_ref[k], 1, 1)
        seen = part * x_ref[:, cols].astype(F32)
        egain_ref[k : k + 1, :] = jnp.sum(seen * factor, axis=0, keepdims=True)
        gain = gain_ref[k : k + 1, :]
        lean += gain * seen
        dh[:, cols] = gain * part
    mean = jnp.sum(lean, axis=-1, keepdims=True) * (1.0 / D)
    pull = factor * factor * factor * mean
    for k in range(KB):
        cols = slice(k * WB, (k + 1) * WB)
        dx_ref[:, cols] = (
            e_ref[:, cols].astype(F32)
            + factor * dh[:, cols]
            - x_ref[:, cols].astype(F32) * pull
        ).astype(BF16)


def params(number):
    return pltpu.CompilerParams(
        collective_id=number, has_side_effects=True, vmem_limit_bytes=56 * 2**20
    )


def exchange_scratch(n, pad):
    return [pltpu.VMEM((n, pad, D), BF16)] * 4, [pltpu.SemaphoreType.DMA((n,))] * 4


def forward(n, x, weights):
    rows = weights[4].shape[0]
    buffers, sems = exchange_scratch(n, rows // n)
    half = jax.ShapeDtypeStruct((BS, D), BF16)
    return pl.pallas_call(
        functools.partial(fwd_kernel, n),
        out_shape=(
            half, half, jax.ShapeDtypeStruct((KB, BS, 2 * WB), BF16), half, half,
            jax.ShapeDtypeStruct((rows, D), BF16), half,
        ),
        in_specs=[VMEM] * 7,
        out_specs=(VMEM,) * 7,
        scratch_shapes=buffers + sems,
        compiler_params=params(0),
        name="layer_forward",
    )(x, *weights)


def backward(n, upstream, x, saved, weights):
    rows = weights[4].shape[0]
    buffers, sems = exchange_scratch(n, rows // n)
    return pl.pallas_call(
        functools.partial(bwd_kernel, n),
        out_shape=(
            jax.ShapeDtypeStruct((BS, D), BF16),
            jax.ShapeDtypeStruct((KB, WB), F32),
            jax.ShapeDtypeStruct((KB, WB, 2 * WB), F32),
            jax.ShapeDtypeStruct((KB, KB, WB), F32),
            jax.ShapeDtypeStruct((KB, KB, WB), F32),
            jax.ShapeDtypeStruct((rows, BS), F32),
            jax.ShapeDtypeStruct((rows, rows), F32),
        ),
        in_specs=[VMEM] * 14,
        out_specs=(VMEM,) * 7,
        scratch_shapes=buffers
        + [
            pltpu.VMEM((KB, BS, 2 * WB), BF16),
            pltpu.VMEM((BS, D), F32),
            pltpu.VMEM((BS, D), F32),
        ]
        + sems,
        compiler_params=params(1),
        name="layer_backward",
    )(upstream, x, *saved, *weights)


def sum_kernel(n, g_ref, out_ref, land, mine, full, ss1, rs1, ss2, rs2):
    me = lax.axis_index("seq")
    greet(n, me)
    greeted(n)
    send_all(n, me, g_ref, land, (ss1, rs1))
    wait_all(n, me, g_ref, land, (ss1, rs1))
    total = land[0].astype(F32)
    for j in range(1, n):
        total = total + land[j].astype(F32)
    mine[0] = total.astype(BF16)

    def give(d, c):
        peer = lax.rem(me + d, n)
        piece(mine, full, (ss2, rs2), 0, peer, me, d).start()
        return c

    lax.fori_loop(1, n, give, 0)
    full[me] = mine[0]

    def take(d, c):
        copy = piece(mine, full, (ss2, rs2), 0, lax.rem(me + d, n), lax.rem(me + n - d, n), d)
        copy.wait_send()
        copy.wait_recv()
        return c

    lax.fori_loop(1, n, take, 0)
    for j in range(n):
        out_ref[j] = full[j].astype(F32)


def sum_over_seq(n, packed):
    each = packed.shape[1]
    return pl.pallas_call(
        functools.partial(sum_kernel, n),
        out_shape=jax.ShapeDtypeStruct((n, each, WB), F32),
        in_specs=[VMEM],
        out_specs=VMEM,
        scratch_shapes=[
            pltpu.VMEM((n, each, WB), BF16),
            pltpu.VMEM((1, each, WB), BF16),
            pltpu.VMEM((n, each, WB), BF16),
        ]
        + [pltpu.SemaphoreType.DMA((n,))] * 4,
        compiler_params=params(2),
        name="gradient_sum",
    )(packed)


def swapped(value):
    return lax.ppermute(value, "section", [(0, 1), (1, 0)])


def on_device(
    fields, cotangent, assignment, norm_gain, value_inner, value_outer,
    gate_inner, gate_outer, seq_inner, seq_outer,
):
    n = lax.axis_size("seq")
    core = lax.axis_index("section")
    is_first = core == 0
    each = BS // n
    pad = max(each, 8)
    rows = n * pad
    inner = jnp.concatenate([value_inner[0], gate_inner[0]], axis=-1)
    raw = (norm_gain[0].reshape(KB, WB), inner, value_outer[0], gate_outer[0], seq_inner[0, 0], seq_outer[0])
    other = tuple(swapped(item) for item in raw)

    def prepared(items):
        gain, inner, vout, gout, sin, sout = items
        sin = jnp.pad(sin.reshape(n, each, BS), ((0, 0), (0, pad - each), (0, 0)))
        eye = jnp.eye(each, dtype=BF16)
        sx = sout.transpose(1, 0, 2)[:, :, :, None] * eye[None, :, None, :]
        sx = jnp.pad(sx, ((0, 0), (0, pad - each), (0, 0), (0, pad - each)))
        return (
            gain, inner, vout.astype(F32), gout.astype(F32),
            sin.reshape(rows, BS), sx.reshape(rows, rows),
        )

    first = prepared(tuple(jnp.where(is_first, a, b) for a, b in zip(raw, other)))
    second = prepared(tuple(jnp.where(is_first, b, a) for a, b in zip(raw, other)))
    x0 = lax.dynamic_index_in_dim(fields, assignment[core], 0, keepdims=False)
    upstream = lax.dynamic_index_in_dim(cotangent, core, 0, keepdims=False)
    x1, *saved0 = forward(n, x0, first)
    last, *saved1 = forward(n, x1, second)
    last_other = swapped(last)
    dx1, *grads1 = backward(n, upstream, x1, saved1, second)
    _, *grads0 = backward(n, dx1, x0, saved0, first)

    def packed(grads):
        egain, ew, evo, ego, esin, esx = grads
        flat = jnp.concatenate(
            [ew[:, :, :WB].reshape(-1, WB), ew[:, :, WB:].reshape(-1, WB),
             evo.reshape(-1, WB), ego.reshape(-1, WB), egain], axis=0)
        size = -(-flat.shape[0] // (16 * n)) * 16
        flat = jnp.pad(flat, ((0, n * size - flat.shape[0]), (0, 0)))
        esx = esx.reshape(n, pad, n, pad)
        eye = jnp.eye(pad, dtype=F32)
        esx = jnp.sum(esx * eye[None, :, None, :], axis=3)[:, :each].transpose(1, 0, 2)
        esin = esin.reshape(n, pad, BS)[:, :each].reshape(BS, BS)
        return flat, esin, esx

    mine1, mine0 = packed(grads1), packed(grads0)

    def joined(zero, one, narrow):
        keep = jnp.where(is_first, zero, one)
        give = jnp.where(is_first, one, zero)
        if narrow:
            return (keep + swapped(give.astype(BF16)).astype(F32)).astype(BF16)
        return keep + swapped(give)

    flat = joined(mine0[0], mine1[0], True)
    esin = joined(mine0[1], mine1[1], False)
    esx = joined(mine0[2], mine1[2], False)
    flat = sum_over_seq(n, flat.reshape(n, -1, WB)).reshape(-1, WB)
    a, b = KB * WB, KB * KB
    final = jnp.where(is_first, jnp.stack([last, last_other]), jnp.stack([last_other, last]))
    return (
        final,
        flat[2 * a + 2 * b : 2 * a + 2 * b + KB].reshape(1, D),
        flat[:a].reshape(1, KB, WB, WB),
        flat[2 * a : 2 * a + b].reshape(1, KB, KB, WB),
        flat[a : 2 * a].reshape(1, KB, WB, WB),
        flat[2 * a + b : 2 * a + 2 * b].reshape(1, KB, KB, WB),
        esin[None, None],
        esx[None],
    )


def solution(mesh):
    in_specs = (
        P(None, "seq", None),
        P(None, "seq", None),
        P(),
        P("section", None),
        P("section", None, None, None),
        P("section", None, None, None),
        P("section", None, None, None),
        P("section", None, None, None),
        P("section", "seq", None, None),
        P("section", "seq", None, None),
    )
    out_specs = (
        P(None, "seq", None),
        P("section", None),
        P("section", None, None, None),
        P("section", None, None, None),
        P("section", None, None, None),
        P("section", None, None, None),
        P("section", "seq", None, None),
        P("section", "seq", None, None),
    )
    return jax.shard_map(
        on_device, mesh=mesh, in_specs=in_specs, out_specs=out_specs, check_vma=False
    )
```

```python
import functools

import jax
import jax.numpy as jnp
from jax import lax
from jax.experimental import pallas as pl
from jax.experimental.pallas import tpu as pltpu
from jax.sharding import PartitionSpec as P

D = 2048
WB = 128
BS = 128
KB = 16
EPSILON = 1e-06
F32 = jnp.float32
BF16 = jnp.bfloat16
MESH = pl.DeviceIdType.MESH
VMEM = pl.BlockSpec(memory_space=pltpu.VMEM)
WIDE = 512
CHUNKS = D // WIDE
PLANE = 4


def dot(a, b, ca, cb):
    return lax.dot_general(a, b, (((ca,), (cb,)), ((), ())), preferred_element_type=F32)


def lane(k):
    return pl.ds(pl.multiple_of(k * WB, WB), WB)


def greet(n, me):
    barrier = pltpu.get_barrier_semaphore()

    def one(d, c):
        pl.semaphore_signal(
            barrier, inc=1, device_id={"seq": lax.rem(me + d, n)}, device_id_type=MESH
        )
        return c

    lax.fori_loop(1, n, one, 0)


def greeted(n):
    pl.semaphore_wait(pltpu.get_barrier_semaphore(), n - 1)


def piece(src, dst, sems, row, to, at, d):
    return pltpu.make_async_remote_copy(
        src_ref=src.at[row],
        dst_ref=dst.at[at],
        send_sem=sems[0].at[d],
        recv_sem=sems[1].at[d],
        device_id={"seq": to},
        device_id_type=MESH,
    )


def send_all(n, me, i, src, dst, sems):
    def one(d, c):
        peer = lax.rem(me + d, n)
        piece(src, dst, sems, (i, peer), peer, (i, me), (i, d)).start()
        return c

    lax.fori_loop(1, n, one, 0)
    dst[i, me] = src[i, me]


def wait_all(n, me, i, src, dst, sems):
    def one(d, c):
        peer = lax.rem(me + d, n)
        origin = lax.rem(me + n - d, n)
        copy = piece(src, dst, sems, (i, peer), peer, (i, origin), (i, d))
        copy.wait_send()
        copy.wait_recv()
        return c

    lax.fori_loop(1, n, one, 0)


def chosen(section, own, other, put):
    core = lax.axis_index("section")

    @pl.when(core == section)
    def _():
        put(own)

    @pl.when(core != section)
    def _():
        put(other)


def load_weights(n, section, own, other, to):
    gain_s, w_s, vo_s, go_s, sin_s, sx_s = to
    rows = sin_s.shape[0]
    pad = rows // n

    def put(refs):
        gain, vin, vout, gin, gout, sin, sout = refs
        gain_s[...] = gain[...]
        vo_s[...] = vout[...].astype(F32)
        go_s[...] = gout[...].astype(F32)
        sin_s[...] = sin[...]
        w_s[:, :, :WB] = vin[...]
        w_s[:, :, WB:] = gin[...]
        wide = dot(sout[...], copies(n, rows), 1, 0)
        sx_s[...] = jnp.where(same_place(rows, pad), wide, 0.0).astype(BF16)

    chosen(section, own, other, put)


def copies(n, rows, dtype=BF16):
    at = lax.broadcasted_iota(jnp.int32, (n, rows), 0)
    to = lax.broadcasted_iota(jnp.int32, (n, rows), 1)
    return jnp.where(to // (rows // n) == at, 1.0, 0.0).astype(dtype)


def same_place(rows, pad):
    at = lax.broadcasted_iota(jnp.int32, (rows, rows), 0)
    to = lax.broadcasted_iota(jnp.int32, (rows, rows), 1)
    return at % pad == to % pad


def cross(read, write, b_ref, back, first=0, last=KB):
    def rows(i, c):
        at = pl.ds(pl.multiple_of(i * 16, 16), 16)
        parts = [read(k, at).astype(F32) for k in range(KB)]
        for l in range(first, last):
            total = None
            for k in range(KB):
                row = b_ref[l, k : k + 1, :] if back else b_ref[k, l : l + 1, :]
                term = parts[k] * row
                total = term if total is None else total + term
            write(l, at, total.astype(BF16))
        return c

    lax.fori_loop(0, BS // 16, rows, 0)


def row_factor(x_ref):
    wide = x_ref[...].astype(F32)
    return lax.rsqrt(jnp.mean(wide * wide, axis=-1, keepdims=True) + EPSILON)


def spread_rows(n, rows, dtype=BF16):
    pad = rows // n
    each = BS // n
    at = lax.broadcasted_iota(jnp.int32, (rows, BS), 0)
    to = lax.broadcasted_iota(jnp.int32, (rows, BS), 1)
    hit = (at // pad * each + at % pad == to) & (at % pad < each)
    return jnp.where(hit, 1.0, 0.0).astype(dtype)


def fwd_kernel(n, section, x_ref, *refs):
    own, other = refs[:7], refs[7:14]
    out_ref, h_ref, t_ref, v_ref, g_ref, sp_ref, s_ref = refs[14:21]
    weights = refs[21:27]
    gain_ref, w_ref, vo_ref, go_ref, sin_ref, sx_ref = weights
    a1, b1, a2, b2, ss1, rs1, ss2, rs2 = refs[27:]
    me = lax.axis_index("seq")
    rows = sin_ref.shape[0]
    pad = rows // n
    greet(n, me)
    load_weights(n, section, own, other, weights)
    factor = row_factor(x_ref)
    for k in range(KB):
        cols = slice(k * WB, (k + 1) * WB)
        gain = gain_ref[k : k + 1, :]
        hidden = (x_ref[:, cols].astype(F32) * factor * gain).astype(BF16)
        h_ref[:, cols] = hidden
        t_ref[k] = dot(hidden, w_ref[k], 1, 0).astype(BF16)

    def put(ref):
        def write(l, at, value):
            ref[at, l * WB : (l + 1) * WB] = value

        return write

    for i in range(CHUNKS):
        each = KB // CHUNKS
        cross(lambda k, at: t_ref[k, at, :WB], put(v_ref), vo_ref, False, i * each, (i + 1) * each)
        y = dot(sin_ref[...], v_ref[:, i * WIDE : (i + 1) * WIDE], 1, 0)
        a1[i] = y.reshape(n, pad, WIDE).astype(BF16)
        if i == 0:
            greeted(n)
        send_all(n, me, i, a1, b1, (ss1, rs1))
    cross(lambda k, at: t_ref[k, at, WB:], put(g_ref), go_ref, False)
    for i in range(CHUNKS):
        wait_all(n, me, i, a1, b1, (ss1, rs1))
        got = b1[i].astype(F32).reshape(rows, WIDE).astype(BF16)
        sp_ref[:, i * WIDE : (i + 1) * WIDE] = got
        y = dot(sx_ref[...], got, 1, 0)
        a2[i] = y.reshape(n, pad, WIDE).astype(BF16)
        send_all(n, me, i, a2, b2, (ss2, rs2))
    for i in range(CHUNKS):
        wait_all(n, me, i, a2, b2, (ss2, rs2))
        cols = slice(i * WIDE, (i + 1) * WIDE)
        mixed = b2[i].astype(F32).reshape(rows, WIDE)
        if rows != BS:
            mixed = dot(spread_rows(n, rows), mixed.astype(BF16), 0, 0)
        s_ref[:, cols] = mixed.astype(BF16)
        out_ref[:, cols] = (
            x_ref[:, cols].astype(F32) + mixed * g_ref[:, cols].astype(F32)
        ).astype(BF16)


def bwd_kernel(n, section, e_ref, x_ref, h_ref, t_ref, v_ref, g_ref, sp_ref, s_ref, *refs):
    own, other = refs[:7], refs[7:14]
    dx_ref, flat_ref, esin_ref, esx_ref = refs[14:18]
    weights = refs[18:24]
    gain_ref, w_ref, vo_ref, go_ref, sin_ref, sx_ref = weights
    a1, b1, a2, b2, dt, up, dh, ss1, rs1, ss2, rs2 = refs[24:]
    me = lax.axis_index("seq")
    rows = sin_ref.shape[0]
    pad = rows // n
    greet(n, me)
    for i in range(CHUNKS):
        cols = slice(i * WIDE, (i + 1) * WIDE)
        ds = e_ref[:, cols].astype(F32) * g_ref[:, cols].astype(F32)
        if rows != BS:
            ds = dot(spread_rows(n, rows), ds.astype(BF16), 1, 0)
        a1[i] = ds.reshape(n, pad, WIDE).astype(BF16)
        if i == 0:
            greeted(n)
        send_all(n, me, i, a1, b1, (ss1, rs1))
    load_weights(n, section, own, other, weights)

    def middle_back(first, b_ref):
        def write(k, at, value):
            dt[k, at, first : first + WB] = value

        cross(lambda l, at: up[at, l * WB : (l + 1) * WB], write, b_ref, True)

    def outer_grad(first, start):
        def block(k, c):
            middle = t_ref[k, :, first : first + WB].astype(F32)
            found = []
            for l in range(KB):
                both = middle * up[:, l * WB : (l + 1) * WB]
                found.append(jnp.sum(both, axis=0, keepdims=True))
            at = pl.ds(pl.multiple_of(start + k * KB, KB), KB)
            flat_ref[at, :] = jnp.concatenate(found, axis=0).astype(BF16)
            return c

        lax.fori_loop(0, KB, block, 0)

    for i in range(CHUNKS):
        cols = slice(i * WIDE, (i + 1) * WIDE)
        dg = e_ref[:, cols].astype(F32) * s_ref[:, cols].astype(F32)
        up[:, cols] = dg.astype(BF16).astype(F32)
    middle_back(WB, go_ref)
    for i in range(CHUNKS):
        wait_all(n, me, i, a1, b1, (ss1, rs1))
        got = b1[i].astype(F32).reshape(rows, WIDE).astype(BF16)
        y = dot(sx_ref[...], got, 0, 0)
        a2[i] = y.reshape(n, pad, WIDE).astype(BF16)
        send_all(n, me, i, a2, b2, (ss2, rs2))
    pairs = jnp.zeros((rows, rows), F32)
    for i in range(CHUNKS):
        got = b1[i].astype(F32).reshape(rows, WIDE).astype(BF16)
        pairs += dot(got, sp_ref[:, i * WIDE : (i + 1) * WIDE], 1, 1)
    esx_ref[...] = lax.dot_general(
        jnp.where(same_place(rows, pad), pairs, 0.0), copies(n, rows, F32),
        (((1,), (1,)), ((), ())), precision=lax.Precision.HIGHEST, preferred_element_type=F32,
    )
    outer_grad(WB, 2 * D + KB * KB)
    inner = jnp.zeros((rows, BS), F32)
    for i in range(CHUNKS):
        wait_all(n, me, i, a2, b2, (ss2, rs2))
        cols = slice(i * WIDE, (i + 1) * WIDE)
        dy = b2[i].astype(F32).reshape(rows, WIDE).astype(BF16)
        inner += dot(dy, v_ref[:, cols], 1, 1)
        up[:, cols] = dot(sin_ref[...], dy, 0, 0).astype(BF16).astype(F32)
    esin_ref[...] = inner
    middle_back(0, vo_ref)
    outer_grad(0, 2 * D)
    factor = row_factor(x_ref)
    lean = jnp.zeros((BS, WB), F32)
    gains = []
    for k in range(KB):
        cols = slice(k * WB, (k + 1) * WB)
        both = dt[k]
        pair = dot(h_ref[:, cols], both, 0, 0).astype(BF16)
        flat_ref[cols, :] = pair[:, :WB]
        flat_ref[D + k * WB : D + (k + 1) * WB, :] = pair[:, WB:]
        part = dot(both, w_ref[k], 1, 1)
        seen = part * x_ref[:, cols].astype(F32)
        gains.append(jnp.sum(seen * factor, axis=0, keepdims=True))
        gain = gain_ref[k : k + 1, :]
        lean += gain * seen
        dh[:, cols] = gain * part
    used = 2 * D + 2 * KB * KB
    flat_ref[used : used + KB, :] = jnp.concatenate(gains, axis=0).astype(BF16)
    left = flat_ref.shape[0] - used - KB
    if left:
        flat_ref[used + KB :, :] = jnp.zeros((left, WB), BF16)
    mean = jnp.sum(lean, axis=-1, keepdims=True) * (1.0 / D)
    pull = factor * factor * factor * mean
    for k in range(KB):
        cols = slice(k * WB, (k + 1) * WB)
        dx_ref[:, cols] = (
            e_ref[:, cols].astype(F32)
            + factor * dh[:, cols]
            - x_ref[:, cols].astype(F32) * pull
        ).astype(BF16)


def params(number):
    return pltpu.CompilerParams(
        collective_id=number, has_side_effects=True, vmem_limit_bytes=56 * 2**20
    )


def weight_scratch(rows):
    return [
        pltpu.VMEM((KB, WB), F32),
        pltpu.VMEM((KB, WB, 2 * WB), BF16),
        pltpu.VMEM((KB, KB, WB), F32),
        pltpu.VMEM((KB, KB, WB), F32),
        pltpu.VMEM((rows, BS), BF16),
        pltpu.VMEM((rows, rows), BF16),
    ]


def exchange_scratch(n, pad):
    return (
        [pltpu.VMEM((CHUNKS, n, pad, WIDE), BF16)] * 4,
        [pltpu.SemaphoreType.DMA((CHUNKS, n))] * 4,
    )


def forward(n, section, x, own, other):
    rows = own[5].shape[0]
    buffers, sems = exchange_scratch(n, rows // n)
    half = jax.ShapeDtypeStruct((BS, D), BF16)
    return pl.pallas_call(
        functools.partial(fwd_kernel, n, section),
        out_shape=(
            half, half, jax.ShapeDtypeStruct((KB, BS, 2 * WB), BF16), half, half,
            jax.ShapeDtypeStruct((rows, D), BF16), half,
        ),
        in_specs=[VMEM] * 15,
        out_specs=(VMEM,) * 7,
        scratch_shapes=weight_scratch(rows) + buffers + sems,
        compiler_params=params(section),
        name="layer_forward",
    )(x, *own, *other)


def backward(n, section, upstream, x, saved, own, other):
    rows = own[5].shape[0]
    buffers, sems = exchange_scratch(n, rows // n)
    return pl.pallas_call(
        functools.partial(bwd_kernel, n, section),
        out_shape=(
            jax.ShapeDtypeStruct((BS, D), BF16),
            jax.ShapeDtypeStruct((n * chunk_rows(n), WB), BF16),
            jax.ShapeDtypeStruct((rows, BS), F32),
            jax.ShapeDtypeStruct((rows, n), F32),
        ),
        in_specs=[VMEM] * 22,
        out_specs=(VMEM,) * 4,
        scratch_shapes=weight_scratch(rows)
        + buffers
        + [
            pltpu.VMEM((KB, BS, 2 * WB), BF16),
            pltpu.VMEM((BS, D), F32),
            pltpu.VMEM((BS, D), F32),
        ]
        + sems,
        compiler_params=params(2 + section),
        name="layer_backward",
    )(upstream, x, *saved, *own, *other)


def chunk_rows(n):
    return -(-(2 * D + 2 * KB * KB + KB) // (16 * n)) * 16


def sum_kernel(n, zero_ref, one_ref, out_ref, give, came, g, land, part, lines, mine, full,
               sc, rc, s1, r1, s2, r2, s3, r3, s4, r4):
    me = lax.axis_index("seq")
    core = lax.axis_index("section")
    depth = n // PLANE
    z, p = me // PLANE, lax.rem(me, PLANE)
    barrier = pltpu.get_barrier_semaphore()
    greet(n, me)
    pl.semaphore_signal(
        barrier, inc=1, device_id={"section": 1 - core}, device_id_type=MESH
    )

    def put(refs):
        give[...] = refs[1][...]
        g[...] = refs[0][...]

    chosen(0, (zero_ref, one_ref), (one_ref, zero_ref), put)
    pl.semaphore_wait(barrier, n)

    def across(q):
        return pltpu.make_async_remote_copy(
            src_ref=give.at[q], dst_ref=came.at[q], send_sem=sc.at[q], recv_sem=rc.at[q],
            device_id={"section": 1 - core}, device_id_type=MESH,
        )

    for q in range(PLANE):
        across(q).start()

    def plane(d, sign=1):
        return lax.rem(p + PLANE + sign * d, PLANE)

    def line(d, sign=1):
        return lax.rem(z + depth + sign * d, depth)

    for q in range(PLANE):
        across(q).wait()
        g[q] = (g[q].astype(F32) + came[q].astype(F32)).astype(BF16)
    for d in range(1, PLANE):
        q = plane(d)
        piece(g, land, (s1, r1), q, z * PLANE + q, p, d).start()
    land[p] = g[p]
    for d in range(1, PLANE):
        q = plane(d)
        copy = piece(g, land, (s1, r1), q, z * PLANE + q, plane(d, -1), d)
        copy.wait_send()
        copy.wait_recv()
    total = land[0].astype(F32)
    for q in range(1, PLANE):
        total = total + land[q].astype(F32)
    part[...] = total.astype(BF16)
    for d in range(1, depth):
        q = line(d)
        piece(part, lines, (s2, r2), q, q * PLANE + p, z, d).start()
    lines[z] = part[z]
    for d in range(1, depth):
        q = line(d)
        copy = piece(part, lines, (s2, r2), q, q * PLANE + p, line(d, -1), d)
        copy.wait_send()
        copy.wait_recv()
    total = lines[0].astype(F32)
    for q in range(1, depth):
        total = total + lines[q].astype(F32)
    mine[0] = total.astype(BF16)
    for d in range(1, depth):
        piece(mine, full, (s3, r3), 0, line(d) * PLANE + p, (p, z), d).start()
    full[p, z] = mine[0]
    for d in range(1, depth):
        copy = piece(mine, full, (s3, r3), 0, line(d) * PLANE + p, (p, line(d, -1)), d)
        copy.wait_send()
        copy.wait_recv()
    for d in range(1, PLANE):
        piece(full, full, (s4, r4), p, z * PLANE + plane(d), p, d).start()
    for d in range(1, PLANE):
        copy = piece(full, full, (s4, r4), p, z * PLANE + plane(d), plane(d, -1), d)
        copy.wait_send()
        copy.wait_recv()
    for q in range(PLANE):
        out_ref[q] = full[q].astype(F32)


def sum_over_seq(n, zero, one):
    each = chunk_rows(n)
    depth = n // PLANE
    whole = pltpu.VMEM((PLANE, depth, each, WB), BF16)
    some = pltpu.VMEM((depth, each, WB), BF16)
    shape = (PLANE, depth, each, WB)
    return pl.pallas_call(
        functools.partial(sum_kernel, n),
        out_shape=jax.ShapeDtypeStruct(shape, F32),
        in_specs=[VMEM] * 2,
        out_specs=VMEM,
        scratch_shapes=[whole] * 4
        + [some, some, pltpu.VMEM((1, each, WB), BF16), whole]
        + [pltpu.SemaphoreType.DMA((PLANE,))] * 4
        + [pltpu.SemaphoreType.DMA((depth,))] * 4
        + [pltpu.SemaphoreType.DMA((PLANE,))] * 2,
        compiler_params=params(4),
        name="gradient_sum",
    )(zero.reshape(shape), one.reshape(shape)).reshape(-1, WB)


def swapped(value):
    return lax.ppermute(value, "section", [(0, 1), (1, 0)])


def on_device(
    fields, cotangent, assignment, norm_gain, value_inner, value_outer,
    gate_inner, gate_outer, seq_inner, seq_outer,
):
    n = lax.axis_size("seq")
    core = lax.axis_index("section")
    is_first = core == 0
    each = BS // n
    pad = max(each, 8)
    rows = n * pad
    sin = jnp.pad(seq_inner[0].reshape(n, each, BS), ((0, 0), (0, pad - each), (0, 0)))
    sout = jnp.pad(seq_outer[0].transpose(1, 0, 2), ((0, 0), (0, pad - each), (0, 0)))
    own = (
        norm_gain[0].reshape(KB, WB), value_inner[0], value_outer[0], gate_inner[0],
        gate_outer[0], sin.reshape(rows, BS), sout.reshape(rows, n),
    )
    other = tuple(swapped(item) for item in own)
    x0 = lax.dynamic_index_in_dim(fields, assignment[core], 0, keepdims=False)
    upstream = lax.dynamic_index_in_dim(cotangent, core, 0, keepdims=False)
    x1, *saved0 = forward(n, 0, x0, own, other)
    last, *saved1 = forward(n, 1, x1, own, other)
    last_other = swapped(last)
    dx1, flat1, esin1, esx1 = backward(n, 1, upstream, x1, saved1, own, other)
    _, flat0, esin0, esx0 = backward(n, 0, dx1, x0, saved0, own, other)

    def joined(zero, one):
        return jnp.where(is_first, zero, one) + swapped(jnp.where(is_first, one, zero))

    esin = joined(esin0, esin1).reshape(n, pad, BS)[:, :each].reshape(BS, BS)
    esx = joined(esx0, esx1).reshape(n, pad, n)[:, :each].transpose(1, 0, 2)
    flat = sum_over_seq(n, flat0, flat1)
    a, b = KB * WB, KB * KB
    final = jnp.where(is_first, jnp.stack([last, last_other]), jnp.stack([last_other, last]))
    return (
        final,
        flat[2 * a + 2 * b : 2 * a + 2 * b + KB].reshape(1, D),
        flat[:a].reshape(1, KB, WB, WB),
        flat[2 * a : 2 * a + b].reshape(1, KB, KB, WB),
        flat[a : 2 * a].reshape(1, KB, WB, WB),
        flat[2 * a + b : 2 * a + 2 * b].reshape(1, KB, KB, WB),
        esin[None, None],
        esx[None],
    )


def solution(mesh):
    in_specs = (
        P(None, "seq", None),
        P(None, "seq", None),
        P(),
        P("section", None),
        P("section", None, None, None),
        P("section", None, None, None),
        P("section", None, None, None),
        P("section", None, None, None),
        P("section", "seq", None, None),
        P("section", "seq", None, None),
    )
    out_specs = (
        P(None, "seq", None),
        P("section", None),
        P("section", None, None, None),
        P("section", None, None, None),
        P("section", None, None, None),
        P("section", None, None, None),
        P("section", "seq", None, None),
        P("section", "seq", None, None),
    )
    return jax.shard_map(
        on_device, mesh=mesh, in_specs=in_specs, out_specs=out_specs, check_vma=False
    )
```

```python
import functools

import jax
import jax.numpy as jnp
from jax import lax
from jax.experimental import pallas as pl
from jax.experimental.pallas import tpu as pltpu
from jax.sharding import PartitionSpec as P

D = 2048
WB = 128
BS = 128
KB = 16
EPSILON = 1e-06
F32 = jnp.float32
BF16 = jnp.bfloat16
MESH = pl.DeviceIdType.MESH
VMEM = pl.BlockSpec(memory_space=pltpu.VMEM)
WIDE = 512
CHUNKS = D // WIDE
PLANE = 4


def dot(a, b, ca, cb):
    return lax.dot_general(a, b, (((ca,), (cb,)), ((), ())), preferred_element_type=F32)


def lane(k):
    return pl.ds(pl.multiple_of(k * WB, WB), WB)


def greet(n, me):
    barrier = pltpu.get_barrier_semaphore()

    def one(d, c):
        pl.semaphore_signal(
            barrier, inc=1, device_id={"seq": lax.rem(me + d, n)}, device_id_type=MESH
        )
        return c

    lax.fori_loop(1, n, one, 0)


def greeted(n):
    pl.semaphore_wait(pltpu.get_barrier_semaphore(), n - 1)


def piece(src, dst, sems, row, to, at, d):
    return pltpu.make_async_remote_copy(
        src_ref=src.at[row],
        dst_ref=dst.at[at],
        send_sem=sems[0].at[d],
        recv_sem=sems[1].at[d],
        device_id={"seq": to},
        device_id_type=MESH,
    )


def send_all(n, me, i, src, dst, sems):
    def one(d, c):
        peer = lax.rem(me + d, n)
        piece(src, dst, sems, (i, peer), peer, (i, me), (i, d)).start()
        return c

    lax.fori_loop(1, n, one, 0)
    dst[i, me] = src[i, me]


def wait_all(n, me, i, src, dst, sems):
    def one(d, c):
        peer = lax.rem(me + d, n)
        origin = lax.rem(me + n - d, n)
        copy = piece(src, dst, sems, (i, peer), peer, (i, origin), (i, d))
        copy.wait_send()
        copy.wait_recv()
        return c

    lax.fori_loop(1, n, one, 0)


def chosen(section, own, other, put):
    core = lax.axis_index("section")

    @pl.when(core == section)
    def _():
        put(own)

    @pl.when(core != section)
    def _():
        put(other)


def load_weights(n, section, own, other, to):
    gain_s, w_s, vo_s, go_s, sin_s, sx_s = to
    rows = sin_s.shape[0]
    pad = rows // n

    def put(refs):
        gain, vin, vout, gin, gout, sin, sout = refs
        gain_s[...] = gain[...]
        vo_s[...] = vout[...].astype(F32)
        go_s[...] = gout[...].astype(F32)
        sin_s[...] = sin[...]
        w_s[:, :, :WB] = vin[...]
        w_s[:, :, WB:] = gin[...]
        wide = dot(sout[...], copies(n, rows), 1, 0)
        sx_s[...] = jnp.where(same_place(rows, pad), wide, 0.0).astype(BF16)

    chosen(section, own, other, put)


def copies(n, rows, dtype=BF16):
    at = lax.broadcasted_iota(jnp.int32, (n, rows), 0)
    to = lax.broadcasted_iota(jnp.int32, (n, rows), 1)
    return jnp.where(to // (rows // n) == at, 1.0, 0.0).astype(dtype)


def same_place(rows, pad):
    at = lax.broadcasted_iota(jnp.int32, (rows, rows), 0)
    to = lax.broadcasted_iota(jnp.int32, (rows, rows), 1)
    return at % pad == to % pad


def cross(read, write, b_ref, back, first=0, last=KB):
    def rows(i, c):
        at = pl.ds(pl.multiple_of(i * 16, 16), 16)
        parts = [read(k, at).astype(F32) for k in range(KB)]
        for l in range(first, last):
            total = None
            for k in range(KB):
                row = b_ref[l, k : k + 1, :] if back else b_ref[k, l : l + 1, :]
                term = parts[k] * row
                total = term if total is None else total + term
            write(l, at, total.astype(BF16))
        return c

    lax.fori_loop(0, BS // 16, rows, 0)


def row_factor(x_ref):
    wide = x_ref[...].astype(F32)
    return lax.rsqrt(jnp.mean(wide * wide, axis=-1, keepdims=True) + EPSILON)


def spread_rows(n, rows, dtype=BF16):
    pad = rows // n
    each = BS // n
    at = lax.broadcasted_iota(jnp.int32, (rows, BS), 0)
    to = lax.broadcasted_iota(jnp.int32, (rows, BS), 1)
    hit = (at // pad * each + at % pad == to) & (at % pad < each)
    return jnp.where(hit, 1.0, 0.0).astype(dtype)


def fwd_kernel(n, section, x_ref, *refs):
    own, other = refs[:7], refs[7:14]
    out_ref, h_ref, t_ref, v_ref, g_ref, sp_ref, s_ref = refs[14:21]
    weights = refs[21:27]
    gain_ref, w_ref, vo_ref, go_ref, sin_ref, sx_ref = weights
    a1, b1, a2, b2, ss1, rs1, ss2, rs2 = refs[27:]
    me = lax.axis_index("seq")
    rows = sin_ref.shape[0]
    pad = rows // n
    greet(n, me)
    load_weights(n, section, own, other, weights)
    factor = row_factor(x_ref)
    for k in range(KB):
        cols = slice(k * WB, (k + 1) * WB)
        gain = gain_ref[k : k + 1, :]
        hidden = (x_ref[:, cols].astype(F32) * factor * gain).astype(BF16)
        h_ref[:, cols] = hidden
        t_ref[k] = dot(hidden, w_ref[k], 1, 0).astype(BF16)

    def put(ref):
        def write(l, at, value):
            ref[at, l * WB : (l + 1) * WB] = value

        return write

    for i in range(CHUNKS):
        each = KB // CHUNKS
        cross(lambda k, at: t_ref[k, at, :WB], put(v_ref), vo_ref, False, i * each, (i + 1) * each)
        y = dot(sin_ref[...], v_ref[:, i * WIDE : (i + 1) * WIDE], 1, 0)
        a1[i] = y.reshape(n, pad, WIDE).astype(BF16)
        if i == 0:
            greeted(n)
        send_all(n, me, i, a1, b1, (ss1, rs1))
    cross(lambda k, at: t_ref[k, at, WB:], put(g_ref), go_ref, False)
    for i in range(CHUNKS):
        wait_all(n, me, i, a1, b1, (ss1, rs1))
        got = b1[i].astype(F32).reshape(rows, WIDE).astype(BF16)
        sp_ref[:, i * WIDE : (i + 1) * WIDE] = got
        y = dot(sx_ref[...], got, 1, 0)
        a2[i] = y.reshape(n, pad, WIDE).astype(BF16)
        send_all(n, me, i, a2, b2, (ss2, rs2))
    for i in range(CHUNKS):
        wait_all(n, me, i, a2, b2, (ss2, rs2))
        cols = slice(i * WIDE, (i + 1) * WIDE)
        mixed = b2[i].astype(F32).reshape(rows, WIDE)
        if rows != BS:
            mixed = dot(spread_rows(n, rows), mixed.astype(BF16), 0, 0)
        s_ref[:, cols] = mixed.astype(BF16)
        out_ref[:, cols] = (
            x_ref[:, cols].astype(F32) + mixed * g_ref[:, cols].astype(F32)
        ).astype(BF16)


def bwd_kernel(n, section, e_ref, x_ref, h_ref, t_ref, v_ref, g_ref, sp_ref, s_ref, *refs):
    own, other = refs[:7], refs[7:14]
    dx_ref, flat_ref, esin_ref, esx_ref = refs[14:18]
    weights = refs[18:24]
    gain_ref, w_ref, vo_ref, go_ref, sin_ref, sx_ref = weights
    a1, b1, a2, b2, dt, up, dh, ss1, rs1, ss2, rs2 = refs[24:]
    me = lax.axis_index("seq")
    rows = sin_ref.shape[0]
    pad = rows // n
    greet(n, me)
    for i in range(CHUNKS):
        cols = slice(i * WIDE, (i + 1) * WIDE)
        ds = e_ref[:, cols].astype(F32) * g_ref[:, cols].astype(F32)
        if rows != BS:
            ds = dot(spread_rows(n, rows), ds.astype(BF16), 1, 0)
        a1[i] = ds.reshape(n, pad, WIDE).astype(BF16)
        if i == 0:
            greeted(n)
        send_all(n, me, i, a1, b1, (ss1, rs1))
    load_weights(n, section, own, other, weights)

    def middle_back(first, b_ref):
        def write(k, at, value):
            dt[k, at, first : first + WB] = value

        cross(lambda l, at: up[at, l * WB : (l + 1) * WB], write, b_ref, True)

    def outer_grad(first, start):
        def block(k, c):
            middle = t_ref[k, :, first : first + WB].astype(F32)
            found = []
            for l in range(KB):
                both = middle * up[:, l * WB : (l + 1) * WB]
                found.append(jnp.sum(both, axis=0, keepdims=True))
            at = pl.ds(pl.multiple_of(start + k * KB, KB), KB)
            flat_ref[at, :] = jnp.concatenate(found, axis=0).astype(BF16)
            return c

        lax.fori_loop(0, KB, block, 0)

    for i in range(CHUNKS):
        cols = slice(i * WIDE, (i + 1) * WIDE)
        dg = e_ref[:, cols].astype(F32) * s_ref[:, cols].astype(F32)
        up[:, cols] = dg.astype(BF16).astype(F32)
    middle_back(WB, go_ref)
    for i in range(CHUNKS):
        wait_all(n, me, i, a1, b1, (ss1, rs1))
        got = b1[i].astype(F32).reshape(rows, WIDE).astype(BF16)
        y = dot(sx_ref[...], got, 0, 0)
        a2[i] = y.reshape(n, pad, WIDE).astype(BF16)
        send_all(n, me, i, a2, b2, (ss2, rs2))
    pairs = jnp.zeros((rows, rows), F32)
    for i in range(CHUNKS):
        got = b1[i].astype(F32).reshape(rows, WIDE).astype(BF16)
        pairs += dot(got, sp_ref[:, i * WIDE : (i + 1) * WIDE], 1, 1)
    esx_ref[...] = lax.dot_general(
        jnp.where(same_place(rows, pad), pairs, 0.0), copies(n, rows, F32),
        (((1,), (1,)), ((), ())), precision=lax.Precision.HIGHEST, preferred_element_type=F32,
    )
    outer_grad(WB, 2 * D + KB * KB)
    inner = jnp.zeros((rows, BS), F32)
    for i in range(CHUNKS):
        wait_all(n, me, i, a2, b2, (ss2, rs2))
        cols = slice(i * WIDE, (i + 1) * WIDE)
        dy = b2[i].astype(F32).reshape(rows, WIDE).astype(BF16)
        inner += dot(dy, v_ref[:, cols], 1, 1)
        up[:, cols] = dot(sin_ref[...], dy, 0, 0).astype(BF16).astype(F32)
    esin_ref[...] = inner
    middle_back(0, vo_ref)
    outer_grad(0, 2 * D)
    factor = row_factor(x_ref)
    lean = jnp.zeros((BS, WB), F32)
    gains = []
    for k in range(KB):
        cols = slice(k * WB, (k + 1) * WB)
        both = dt[k]
        pair = dot(h_ref[:, cols], both, 0, 0).astype(BF16)
        flat_ref[cols, :] = pair[:, :WB]
        flat_ref[D + k * WB : D + (k + 1) * WB, :] = pair[:, WB:]
        part = dot(both, w_ref[k], 1, 1)
        seen = part * x_ref[:, cols].astype(F32)
        gains.append(jnp.sum(seen * factor, axis=0, keepdims=True))
        gain = gain_ref[k : k + 1, :]
        lean += gain * seen
        dh[:, cols] = gain * part
    used = 2 * D + 2 * KB * KB
    flat_ref[used : used + KB, :] = jnp.concatenate(gains, axis=0).astype(BF16)
    left = flat_ref.shape[0] - used - KB
    if left:
        flat_ref[used + KB :, :] = jnp.zeros((left, WB), BF16)
    mean = jnp.sum(lean, axis=-1, keepdims=True) * (1.0 / D)
    pull = factor * factor * factor * mean
    for k in range(KB):
        cols = slice(k * WB, (k + 1) * WB)
        dx_ref[:, cols] = (
            e_ref[:, cols].astype(F32)
            + factor * dh[:, cols]
            - x_ref[:, cols].astype(F32) * pull
        ).astype(BF16)


def params(number):
    return pltpu.CompilerParams(
        collective_id=number, has_side_effects=True, vmem_limit_bytes=56 * 2**20
    )


def weight_scratch(rows):
    return [
        pltpu.VMEM((KB, WB), F32),
        pltpu.VMEM((KB, WB, 2 * WB), BF16),
        pltpu.VMEM((KB, KB, WB), F32),
        pltpu.VMEM((KB, KB, WB), F32),
        pltpu.VMEM((rows, BS), BF16),
        pltpu.VMEM((rows, rows), BF16),
    ]


def exchange_scratch(n, pad):
    return (
        [pltpu.VMEM((CHUNKS, n, pad, WIDE), BF16)] * 4,
        [pltpu.SemaphoreType.DMA((CHUNKS, n))] * 4,
    )


def forward(n, section, x, own, other):
    rows = own[5].shape[0]
    buffers, sems = exchange_scratch(n, rows // n)
    half = jax.ShapeDtypeStruct((BS, D), BF16)
    return pl.pallas_call(
        functools.partial(fwd_kernel, n, section),
        out_shape=(
            half, half, jax.ShapeDtypeStruct((KB, BS, 2 * WB), BF16), half, half,
            jax.ShapeDtypeStruct((rows, D), BF16), half,
        ),
        in_specs=[VMEM] * 15,
        out_specs=(VMEM,) * 7,
        scratch_shapes=weight_scratch(rows) + buffers + sems,
        compiler_params=params(section),
        name="layer_forward",
    )(x, *own, *other)


def backward(n, section, upstream, x, saved, own, other):
    rows = own[5].shape[0]
    buffers, sems = exchange_scratch(n, rows // n)
    return pl.pallas_call(
        functools.partial(bwd_kernel, n, section),
        out_shape=(
            jax.ShapeDtypeStruct((BS, D), BF16),
            jax.ShapeDtypeStruct((n * chunk_rows(n), WB), BF16),
            jax.ShapeDtypeStruct((rows, BS), F32),
            jax.ShapeDtypeStruct((rows, n), F32),
        ),
        in_specs=[VMEM] * 22,
        out_specs=(VMEM,) * 4,
        scratch_shapes=weight_scratch(rows)
        + buffers
        + [
            pltpu.VMEM((KB, BS, 2 * WB), BF16),
            pltpu.VMEM((BS, D), F32),
            pltpu.VMEM((BS, D), F32),
        ]
        + sems,
        compiler_params=params(2 + section),
        name="layer_backward",
    )(upstream, x, *saved, *own, *other)


def chunk_rows(n):
    return -(-(2 * D + 2 * KB * KB + KB) // (16 * n)) * 16


def sum_kernel(n, zero_ref, one_ref, *refs):
    outs = refs[:5]
    give, came, g, land, part, lines, mine, full = refs[5:13]
    sc, rc, s1, r1, s2, r2, s3, r3, s4, r4 = refs[13:]
    me = lax.axis_index("seq")
    core = lax.axis_index("section")
    depth = n // PLANE
    z, p = me // PLANE, lax.rem(me, PLANE)
    barrier = pltpu.get_barrier_semaphore()
    greet(n, me)
    pl.semaphore_signal(
        barrier, inc=1, device_id={"section": 1 - core}, device_id_type=MESH
    )

    def put(refs):
        give[...] = refs[1][...]
        g[...] = refs[0][...]

    chosen(0, (zero_ref, one_ref), (one_ref, zero_ref), put)
    pl.semaphore_wait(barrier, n)

    def plane(d, sign=1):
        return lax.rem(p + PLANE + sign * d, PLANE)

    def line(d, sign=1):
        return lax.rem(z + depth + sign * d, depth)

    def across(q, at):
        return pltpu.make_async_remote_copy(
            src_ref=give.at[q, at], dst_ref=came.at[q, at],
            send_sem=sc.at[q, at], recv_sem=rc.at[q, at],
            device_id={"section": 1 - core}, device_id_type=MESH,
        )

    for e in range(1, depth + 1):
        for q in range(PLANE):
            across(q, line(e)).start()
    for e in range(1, depth + 1):
        at = line(e)
        for q in range(PLANE):
            across(q, at).wait()
            g[q, at] = (g[q, at].astype(F32) + came[q, at].astype(F32)).astype(BF16)
        for d in range(1, PLANE):
            q = plane(d)
            piece(g, land, (s1, r1), (q, at), z * PLANE + q, (p, at), (d, e - 1)).start()
        land[p, at] = g[p, at]
    for e in range(1, depth + 1):
        at = line(e)
        for d in range(1, PLANE):
            q = plane(d)
            copy = piece(
                g, land, (s1, r1), (q, at), z * PLANE + q, (plane(d, -1), at), (d, e - 1)
            )
            copy.wait_send()
            copy.wait_recv()
        total = land[0, at].astype(F32)
        for q in range(1, PLANE):
            total = total + land[q, at].astype(F32)
        part[at] = total.astype(BF16)
        if e < depth:
            piece(part, lines, (s2, r2), at, at * PLANE + p, z, e).start()
    lines[z] = part[z]
    for d in range(1, depth):
        q = line(d)
        copy = piece(part, lines, (s2, r2), q, q * PLANE + p, line(d, -1), d)
        copy.wait_send()
        copy.wait_recv()
    total = lines[0].astype(F32)
    for q in range(1, depth):
        total = total + lines[q].astype(F32)
    mine[0] = total.astype(BF16)
    for d in range(1, depth):
        piece(mine, full, (s3, r3), 0, line(d) * PLANE + p, (p, z), d).start()
    for d in range(1, PLANE):
        piece(mine, full, (s4, r4), 0, z * PLANE + plane(d), (p, z), (d, 0)).start()
    full[p, z] = mine[0]
    for e in range(1, depth):
        at = line(e, -1)
        copy = piece(mine, full, (s3, r3), 0, line(e) * PLANE + p, (p, at), e)
        copy.wait_send()
        copy.wait_recv()
        for d in range(1, PLANE):
            piece(full, full, (s4, r4), (p, at), z * PLANE + plane(d), (p, at), (d, e)).start()
    for e in range(depth):
        at = line(e, -1)
        for d in range(1, PLANE):
            copy = piece(
                full, full, (s4, r4), (p, at), z * PLANE + plane(d), (plane(d, -1), at), (d, e)
            )
            copy.wait_send()
            copy.wait_recv()
    each = full.shape[2]
    for j in range(n):
        start = 0
        for ref in outs:
            low, high = max(j * each, start), min((j + 1) * each, start + ref.shape[0])
            if low < high:
                ref[low - start : high - start, :] = full[
                    j // depth, j % depth, low - j * each : high - j * each, :
                ].astype(F32)
            start += ref.shape[0]


def sum_over_seq(n, zero, one):
    each = chunk_rows(n)
    depth = n // PLANE
    whole = pltpu.VMEM((PLANE, depth, each, WB), BF16)
    some = pltpu.VMEM((depth, each, WB), BF16)
    shape = (PLANE, depth, each, WB)
    return pl.pallas_call(
        functools.partial(sum_kernel, n),
        out_shape=tuple(
            jax.ShapeDtypeStruct((size, WB), F32) for size in (D, D, KB * KB, KB * KB, KB)
        ),
        in_specs=[VMEM] * 2,
        out_specs=(VMEM,) * 5,
        scratch_shapes=[whole] * 4
        + [some, some, pltpu.VMEM((1, each, WB), BF16), whole]
        + [pltpu.SemaphoreType.DMA((PLANE, depth))] * 4
        + [pltpu.SemaphoreType.DMA((depth,))] * 4
        + [pltpu.SemaphoreType.DMA((PLANE, depth))] * 2,
        compiler_params=params(4),
        name="gradient_sum",
    )(zero.reshape(shape), one.reshape(shape))


def swapped(value):
    return lax.ppermute(value, "section", [(0, 1), (1, 0)])


def on_device(
    fields, cotangent, assignment, norm_gain, value_inner, value_outer,
    gate_inner, gate_outer, seq_inner, seq_outer,
):
    n = lax.axis_size("seq")
    core = lax.axis_index("section")
    is_first = core == 0
    each = BS // n
    pad = max(each, 8)
    rows = n * pad
    sin = jnp.pad(seq_inner[0].reshape(n, each, BS), ((0, 0), (0, pad - each), (0, 0)))
    sout = jnp.pad(seq_outer[0].transpose(1, 0, 2), ((0, 0), (0, pad - each), (0, 0)))
    own = (
        norm_gain[0].reshape(KB, WB), value_inner[0], value_outer[0], gate_inner[0],
        gate_outer[0], sin.reshape(rows, BS), sout.reshape(rows, n),
    )
    other = tuple(swapped(item) for item in own)
    x0 = lax.dynamic_index_in_dim(fields, assignment[core], 0, keepdims=False)
    upstream = lax.dynamic_index_in_dim(cotangent, core, 0, keepdims=False)
    x1, *saved0 = forward(n, 0, x0, own, other)
    last, *saved1 = forward(n, 1, x1, own, other)
    last_other = swapped(last)
    dx1, flat1, esin1, esx1 = backward(n, 1, upstream, x1, saved1, own, other)
    _, flat0, esin0, esx0 = backward(n, 0, dx1, x0, saved0, own, other)

    def joined(zero, one):
        return jnp.where(is_first, zero, one) + swapped(jnp.where(is_first, one, zero))

    esin = joined(esin0, esin1).reshape(n, pad, BS)[:, :each].reshape(BS, BS)
    esx = joined(esx0, esx1).reshape(n, pad, n)[:, :each].transpose(1, 0, 2)
    vin, gin, vout, gout, gain = sum_over_seq(n, flat0, flat1)
    final = jnp.where(is_first, jnp.stack([last, last_other]), jnp.stack([last_other, last]))
    return (
        final,
        gain.reshape(1, D),
        vin.reshape(1, KB, WB, WB),
        vout.reshape(1, KB, KB, WB),
        gin.reshape(1, KB, WB, WB),
        gout.reshape(1, KB, KB, WB),
        esin[None, None],
        esx[None],
    )


def solution(mesh):
    in_specs = (
        P(None, "seq", None),
        P(None, "seq", None),
        P(),
        P("section", None),
        P("section", None, None, None),
        P("section", None, None, None),
        P("section", None, None, None),
        P("section", None, None, None),
        P("section", "seq", None, None),
        P("section", "seq", None, None),
    )
    out_specs = (
        P(None, "seq", None),
        P("section", None),
        P("section", None, None, None),
        P("section", None, None, None),
        P("section", None, None, None),
        P("section", None, None, None),
        P("section", "seq", None, None),
        P("section", "seq", None, None),
    )
    return jax.shard_map(
        on_device, mesh=mesh, in_specs=in_specs, out_specs=out_specs, check_vma=False
    )
```
